32 devices in a mesh: fsdp: 16 (over z, x, core), seq: 2 (over y).
Axes of the slice: x: 2, y: 2, z: 4, core: 2. Of those that a mesh axis runs over, the one named last changes fastest.
Arguments:
- tokens: bfloat16 [16, 1024, 1024], P('fsdp', 'seq'), may hold values from -6 to 6
- teacher: bfloat16 [16, 1024, 1024], P('fsdp', 'seq'), may hold values from -6 to 6
- out_grad: bfloat16 [16, 1024, 1024], P('fsdp', 'seq'), may hold values from -8 to 8
- validity: int32 [16, 1024], P('fsdp', 'seq'), may hold values from 0 to 1, as said below
- loss_grad: float32 [], replicated, may hold values from 85 to 170
- ln1_gain: bfloat16 [1024], P('fsdp'), may hold values from 0.5 to 1.5
- ln1_bias: bfloat16 [1024], P('fsdp'), may hold values from -3 to 3
- qkv_weight: bfloat16 [1024, 3072], P('fsdp'), may hold values from -0.1875 to 0.1875
- qv_bias: bfloat16 [2, 1024], P(None, 'fsdp'), may hold values from -3 to 3
- proj_weight: bfloat16 [1024, 1024], P('fsdp'), may hold values from -0.75 to 0.75
- proj_bias: bfloat16 [1024], P('fsdp'), may hold values from -3 to 3
- ln2_gain: bfloat16 [1024], P('fsdp'), may hold values from 0.5 to 1.5
- ln2_bias: bfloat16 [1024], P('fsdp'), may hold values from -3 to 3
- fc1_weight: bfloat16 [1024, 4096], P('fsdp'), may hold values from -0.1875 to 0.1875
- fc1_bias: bfloat16 [4096], P('fsdp'), may hold values from -3 to 3
- fc2_weight: bfloat16 [4096, 1024], P('fsdp'), may hold values from -0.09375 to 0.09375
- fc2_bias: bfloat16 [1024], P('fsdp'), may hold values from -3 to 3
Outputs:
- loss: float32 [], replicated
- layer_out: bfloat16 [16, 1024, 1024], P('fsdp', 'seq')
- input_grad: bfloat16 [16, 1024, 1024], P('fsdp', 'seq')
- ln1_gain_grad: float32 [1024], P('fsdp')
- ln1_bias_grad: float32 [1024], P('fsdp')
- qkv_weight_grad: float32 [1024, 3072], P('fsdp')
- qv_bias_grad: float32 [2, 1024], P(None, 'fsdp')
- proj_weight_grad: float32 [1024, 1024], P('fsdp')
- proj_bias_grad: float32 [1024], P('fsdp')
- ln2_gain_grad: float32 [1024], P('fsdp')
- ln2_bias_grad: float32 [1024], P('fsdp')
- fc1_weight_grad: float32 [1024, 4096], P('fsdp')
- fc1_bias_grad: float32 [4096], P('fsdp')
- fc2_weight_grad: float32 [4096, 1024], P('fsdp')
- fc2_bias_grad: float32 [1024], P('fsdp')
The draws below stay inside these ranges and needn't reach their ends.
Inputs may be any that keep to these rules, and one draw needn't show every extreme that they name: `validity`: each slot is either empty (all zero) or holds a clip whose valid tokens form a prefix of 512 tokens or more; 10 of the 16 slots hold clips.
All inputs are finite; a program needn't handle non-finite values.
Results may differ from the reference program's by a relative error of at most 0.01.
Values may be sent and summed in bfloat16 or wider, within the bound.
No kernel may reach another device: no remote copies, remote signals or barrier semaphores. Data moves between devices by JAX's collectives and lax.ppermute only.
A program may use at most 192 MiB of HBM per device.

```python
import jax
import jax.numpy as jnp
from jax import lax

D = 1024
H = 16
DH = 64
FF = 4096
LEN = 1024
CLIP_DEV = 1
SLOTS = 16
REAL_CLIPS = 10


def draw_validity(key, part):
    slot_key = jax.random.fold_in(key, 11)
    length_key = jax.random.fold_in(key, 12)
    chosen_key = jax.random.fold_in(key, 13)
    slot_order = jax.random.permutation(slot_key, SLOTS)
    chosen = jax.random.randint(chosen_key, (), 0, SLOTS // CLIP_DEV)
    on_chosen = jnp.arange(SLOTS) // CLIP_DEV == chosen
    priority = jnp.where(on_chosen, slot_order - SLOTS, slot_order)
    ranking = jnp.argsort(jnp.argsort(priority))
    lengths = jax.random.randint(length_key, (SLOTS,), LEN // 2, LEN + 1)
    lengths = jnp.where(on_chosen, LEN, lengths)
    lengths = jnp.where(ranking < REAL_CLIPS, lengths, 0)
    position = jnp.arange(LEN)[None, :]
    return (position < lengths[:, None]).astype(jnp.int32)


def shared_tokens(key):
    token_key = jax.random.fold_in(key, 21)
    values = jax.random.normal(token_key, (SLOTS, LEN, D), jnp.float32)
    return jnp.clip(values, -6.0, 6.0)


def draw_tokens(key, part):
    return shared_tokens(key).astype(jnp.bfloat16)


def draw_out_grad(key, part):
    base = shared_tokens(key)
    noise_key = jax.random.fold_in(key, 22)
    pair_key = jax.random.fold_in(key, 23)
    noise = jax.random.normal(noise_key, (SLOTS, LEN, D), jnp.float32)
    blocks = SLOTS // CLIP_DEV
    block_width = D // blocks
    pairing = jax.random.permutation(pair_key, blocks)
    slot_block = jnp.arange(SLOTS) // CLIP_DEV
    feature_block = jnp.arange(D) // block_width
    paired = pairing[slot_block][:, None] == feature_block[None, :]
    factor = jnp.where(paired, 4.0, 1.0).astype(jnp.float32)[:, None, :]
    return jnp.clip(1.5 * base + 0.5 * noise * factor, -8.0, 8.0).astype(jnp.bfloat16)


def levels(rng, shape, cuts, low, high):
    def one(axis_at, blocks):
        heights = jax.random.uniform(jax.random.fold_in(jax.random.fold_in(rng, 6), axis_at), (blocks,), jnp.float32, low / len(cuts), high / len(cuts))
        return jnp.repeat(jnp.exp(heights), shape[axis_at] // blocks).reshape((-1,) + (1,) * (len(shape) - axis_at - 1))

    level = one(*cuts[0])
    for cut in cuts[1:]:
        level = level * one(*cut)
    return level


def scatter_about(key, shape, spread, most, shards=(), dtype=jnp.bfloat16):
    result = jax.random.normal(key, shape, jnp.float32) * spread
    if len(shards) > 0:
        result = levels(key, shape, shards, -0.22, 0.18) * result
    return jnp.clip(result, min=-most, max=most).astype(dtype)


def setup_inputs(seed: int = 0) -> dict:
    seeds = jax.random.split(jax.random.key(seed), 18)
    return {
        "tokens": draw_tokens(jax.random.fold_in(seeds[17], 71), 0),
        "teacher": scatter_about(seeds[1], (SLOTS, LEN, D), 1.0, 6.0, ((0, 16), (1, 2))),
        "out_grad": draw_out_grad(jax.random.fold_in(seeds[17], 71), 0),
        "validity": draw_validity(jax.random.fold_in(seeds[17], 71), 0),
        "loss_grad": jnp.clip(jax.random.uniform(seeds[4], (), jnp.float32, 85.0, 170.0), 85.0, 170.0),
        "ln1_gain": jnp.clip(1.0 + 0.1 * jax.random.normal(seeds[5], (D,), jnp.float32), 0.5, 1.5).astype(jnp.bfloat16),
        "ln1_bias": scatter_about(seeds[6], (D,), 0.5, 3.0, ((0, 16),)),
        "qkv_weight": scatter_about(seeds[7], (D, 3 * D), D ** -0.5, 0.1875, ((0, 16),)),
        "qv_bias": scatter_about(seeds[8], (2, D), 0.5, 3.0, ((1, 16),)),
        "proj_weight": scatter_about(seeds[9], (D, D), (max(D // 16, 1)) ** -0.5, 0.75, ((0, 16),)),
        "proj_bias": scatter_about(seeds[10], (D,), 0.5, 3.0, ((0, 16),)),
        "ln2_gain": jnp.clip(1.0 + 0.1 * jax.random.normal(seeds[11], (D,), jnp.float32), 0.5, 1.5).astype(jnp.bfloat16),
        "ln2_bias": scatter_about(seeds[12], (D,), 0.5, 3.0, ((0, 16),)),
        "fc1_weight": scatter_about(seeds[13], (D, FF), D ** -0.5, 0.1875, ((0, 16),)),
        "fc1_bias": scatter_about(seeds[14], (FF,), 0.5, 3.0, ((0, 16),)),
        "fc2_weight": scatter_about(seeds[15], (FF, D), FF ** -0.5, 0.09375, ((0, 16),)),
        "fc2_bias": scatter_about(seeds[16], (D,), 0.5, 3.0, ((0, 16),)),
    }


@jax.custom_vjp
def low(v):
    return lax.optimization_barrier(v.astype(jnp.bfloat16)).astype(jnp.float32)

@jax.custom_vjp
def low_back(v):
    return v

def low_keep(v):
    return (low(v), None)

def low_pass(kept, grad):
    return (grad,)

def back_keep(v):
    return (v, None)

def back_low(kept, grad):
    return (low(grad),)
low.defvjp(low_keep, low_pass)
low_back.defvjp(back_keep, back_low)
epsilon = 1e-06
mask_depth = 1000.0
root_half = 0.7071067811865476

def product(left, right):
    return jnp.dot(left, right, precision=lax.Precision.HIGHEST, preferred_element_type=jnp.float32)

def layer_norm(matrix, gain_row, offset):
    average = lax.optimization_barrier(jnp.mean(matrix, axis=-1, keepdims=True))
    centred = matrix - average
    variance = lax.optimization_barrier(jnp.mean(centred * centred, axis=-1, keepdims=True))
    return centred * lax.rsqrt(variance + epsilon) * gain_row + offset

def one_clip(params, clip_rows, clip_valid):
    gain_one, bias_one, qkv_w, qv_b, proj_w, proj_b, gain_two, bias_two, fc1_w, fc1_b, fc2_w, fc2_b = params
    length = clip_rows.shape[0]
    normed = low(layer_norm(clip_rows, gain_one, bias_one))
    bias_full = jnp.concatenate([qv_b[0], jnp.zeros_like(qv_b[0]), qv_b[1]])
    mixed = low_back(low(product(normed, qkv_w) + bias_full))
    query = mixed[:, :D].reshape(length, H, DH).transpose(1, 0, 2)
    key_rows = mixed[:, D:2 * D].reshape(length, H, DH).transpose(1, 0, 2)
    value_rows = mixed[:, 2 * D:].reshape(length, H, DH).transpose(1, 0, 2)
    key_bias = (clip_valid - 1.0) * mask_depth
    scores = low_back(jnp.einsum('hqd,hkd->hqk', query, key_rows, precision=lax.Precision.HIGHEST) * DH ** (-0.5))
    scores = scores + key_bias[None, None, :]
    highest = lax.optimization_barrier(jnp.max(scores, axis=-1, keepdims=True))
    exponent = jnp.exp(scores - highest)
    weights_p = exponent / lax.optimization_barrier(jnp.sum(exponent, axis=-1, keepdims=True))
    attended = jnp.einsum('hqk,hkd->hqd', low(weights_p), value_rows, precision=lax.Precision.HIGHEST)
    attended = low_back(low(attended.transpose(1, 0, 2).reshape(length, D)))
    branch = low_back(product(attended, proj_w) + proj_b)
    resid = clip_rows + branch
    hidden_in = low(layer_norm(resid, gain_two, bias_two))
    upper = low_back(product(hidden_in, fc1_w) + fc1_b)
    active = low(0.5 * upper * (1.0 + lax.erf(upper * root_half)))
    branch_two = low_back(product(active, fc2_w) + fc2_b)
    return clip_valid[:, None] * (resid + branch_two)

def forward(params, inputs, valid_f, teacher_f, count):

    def clip_step(carried, pieces):
        clip_rows, clip_valid = pieces
        return (carried, jax.checkpoint(one_clip)(params, clip_rows, clip_valid))
    _, outputs = lax.scan(clip_step, jnp.zeros((), jnp.float32), (inputs, valid_f))
    error = outputs - teacher_f
    loss = jnp.sum(valid_f[:, :, None] * error * error) / count
    return (outputs, loss)

def reference(tokens, teacher, out_grad, validity, loss_grad, ln1_gain, ln1_bias, qkv_weight, qv_bias, proj_weight, proj_bias, ln2_gain, ln2_bias, fc1_weight, fc1_bias, fc2_weight, fc2_bias):
    params = tuple((w.astype(jnp.float32) for w in (ln1_gain, ln1_bias, qkv_weight, qv_bias, proj_weight, proj_bias, ln2_gain, ln2_bias, fc1_weight, fc1_bias, fc2_weight, fc2_bias)))
    inputs = tokens.astype(jnp.float32)
    teacher_f = teacher.astype(jnp.float32)
    valid_f = validity.astype(jnp.float32)
    count = jnp.sum(valid_f)

    def wrapped(weights, values):
        return forward(weights, values, valid_f, teacher_f, count)
    (outputs, loss), pullback = jax.vjp(wrapped, params, inputs)
    grads, input_grad = pullback((out_grad.astype(jnp.float32), loss_grad.astype(jnp.float32)))
    return (loss, outputs.astype(jnp.bfloat16), input_grad.astype(jnp.bfloat16), grads[0], grads[1], grads[2], grads[3], grads[4], grads[5], grads[6], grads[7], grads[8], grads[9], grads[10], grads[11])
```

```python
import jax
import jax.numpy as jnp
from jax import lax
from jax.experimental import pallas as pl
from jax.experimental.pallas import tpu as pltpu
from jax.sharding import PartitionSpec as P

LANES=128

DH=64
def lane_of(n): return lax.broadcasted_iota(jnp.int32,(n,LANES),1)
NT=(((1,),(1,)),((),()))
NN=(((1,),(0,)),((),()))
def mm(a,b,d): return lax.dot_general(a,b,d,preferred_element_type=jnp.float32)

def split3(col):
    hi=col.astype(jnp.bfloat16).astype(jnp.float32)
    rest=col-hi
    mid=rest.astype(jnp.bfloat16).astype(jnp.float32)
    return hi,mid,rest-mid

def key_side(k,kb,lane,h):
    base=DH*(1-h)
    extra=jnp.where(lane==base,kb,jnp.where((lane>base)&(lane<base+4),1.0,0.0))
    return jnp.where(lane//DH==h,k,extra).astype(jnp.bfloat16)

def fwd_kernel(q_ref,k_ref,v_ref,kb_ref,o_ref,qa_ref,*,chunk):
    nq=q_ref.shape[0]; nk=k_ref.shape[0]
    lane_k=lane_of(nk); lane_q=lane_of(chunk)
    k=k_ref[...].astype(jnp.float32); v=v_ref[...].astype(jnp.float32); kb=kb_ref[...].astype(jnp.float32)
    keys=[key_side(k,kb,lane_k,h) for h in (0,1)]
    vals=[jnp.where(lane_k//DH==h,v,jnp.where(lane_k==DH*(1-h),1.0,0.0)).astype(jnp.bfloat16) for h in (0,1)]
    for c in range(nq//chunk):
        rows=pl.ds(c*chunk,chunk)
        q=q_ref[rows,:].astype(jnp.float32)*0.125
        outs=[]
        for h in (0,1):
            base=DH*(1-h)
            inh=lane_q//DH==h
            qh=jnp.where(inh,q,jnp.where(lane_q==base,1.0,0.0))
            s=mm(qh.astype(jnp.bfloat16),keys[h],NT)
            m=jnp.max(s,axis=1,keepdims=True)
            p=jnp.exp(s-m).astype(jnp.bfloat16)
            o=mm(p,vals[h],NN)
            l=o[:,base:base+1]
            outs.append(o/l)
            hi,mid,lo=split3(m+jnp.log(l))
            qa=jnp.where(lane_q==base+1,-hi,jnp.where(lane_q==base+2,-mid,jnp.where(lane_q==base+3,-lo,qh)))
            qa_ref[rows,h*LANES:(h+1)*LANES]=qa.astype(jnp.bfloat16)
        o_ref[rows,:]=jnp.where(lane_q<DH,outs[0],outs[1]).astype(jnp.bfloat16)

def bwd_kernel(qa_ref,k_ref,v_ref,kb_ref,do_ref,o_ref,dq_ref,dk_ref,dv_ref,*,chunk):
    nq=do_ref.shape[0]; nk=k_ref.shape[0]
    lane_q=lane_of(nq); lane_k=lane_of(chunk)
    do=do_ref[...].astype(jnp.float32)
    prod=do*o_ref[...].astype(jnp.float32)
    dos=[];
    for h in (0,1):
        base=DH*(1-h)
        inh=lane_q//DH==h
        d=jnp.sum(jnp.where(inh,prod,0.0),axis=1,keepdims=True)
        hi,mid,lo=split3(d)
        dos.append(jnp.where(inh,do,jnp.where(lane_q==base,-hi,jnp.where(lane_q==base+1,-mid,jnp.where(lane_q==base+2,-lo,0.0)))).astype(jnp.bfloat16))
    dq=[None,None]
    for c in range(nk//chunk):
        rows=pl.ds(c*chunk,chunk)
        k=k_ref[rows,:].astype(jnp.float32); v=v_ref[rows,:].astype(jnp.float32); kb=kb_ref[rows,:].astype(jnp.float32)
        kt=k.T.astype(jnp.bfloat16)
        dks=[];dvs=[]
        for h in (0,1):
            base=DH*(1-h)
            inh=lane_k//DH==h
            qa=qa_ref[:,h*LANES:(h+1)*LANES]
            ka=key_side(k,kb,lane_k,h)
            va=jnp.where(inh,v,jnp.where((lane_k>=base)&(lane_k<base+3),1.0,0.0)).astype(jnp.bfloat16)
            p=jnp.exp(mm(ka,qa,NT))
            dp=mm(va,dos[h],NT)
            ds=(p*dp).astype(jnp.bfloat16)
            dvs.append(mm(p.astype(jnp.bfloat16),dos[h],NN))
            dks.append(mm(ds,qa,NN))
            part=mm(kt[h*DH:(h+1)*DH,:],ds,NN)
            dq[h]=part if dq[h] is None else dq[h]+part
        dk_ref[rows,:]=jnp.where(lane_k<DH,dks[0],dks[1]).astype(jnp.bfloat16)
        dv_ref[rows,:]=jnp.where(lane_k<DH,dvs[0],dvs[1]).astype(jnp.bfloat16)
    for h in (0,1):
        dq_ref[h*DH:(h+1)*DH,:]=(dq[h]*0.125).astype(jnp.bfloat16)

def attn_fwd(q,k,v,kb,interpret=False):
    nq,width=q.shape; nk=k.shape[0]; pairs=width//LANES
    chunk=min(256,nq)
    return pl.pallas_call(lambda *r:fwd_kernel(*r,chunk=chunk),grid=(pairs,),
      in_specs=[pl.BlockSpec((nq,LANES),lambda i:(0,i)),pl.BlockSpec((nk,LANES),lambda i:(0,i)),pl.BlockSpec((nk,LANES),lambda i:(0,i)),pl.BlockSpec((nk,LANES),lambda i:(0,0))],
      out_specs=[pl.BlockSpec((nq,LANES),lambda i:(0,i)),pl.BlockSpec((nq,2*LANES),lambda i:(0,i))],
      out_shape=[jax.ShapeDtypeStruct((nq,width),jnp.bfloat16),jax.ShapeDtypeStruct((nq,2*width),jnp.bfloat16)],interpret=interpret)(q,k,v,kb)

def attn_bwd(qa,k,v,kb,do,o,interpret=False):
    nq,width=do.shape; nk=k.shape[0]; pairs=width//LANES
    chunk=min(256,nk)
    return pl.pallas_call(lambda *r:bwd_kernel(*r,chunk=chunk),grid=(pairs,),
      in_specs=[pl.BlockSpec((nq,2*LANES),lambda i:(0,i)),pl.BlockSpec((nk,LANES),lambda i:(0,i)),pl.BlockSpec((nk,LANES),lambda i:(0,i)),pl.BlockSpec((nk,LANES),lambda i:(0,0)),pl.BlockSpec((nq,LANES),lambda i:(0,i)),pl.BlockSpec((nq,LANES),lambda i:(0,i))],
      out_specs=[pl.BlockSpec((LANES,nq),lambda i:(i,0)),pl.BlockSpec((nk,LANES),lambda i:(0,i)),pl.BlockSpec((nk,LANES),lambda i:(0,i))],
      out_shape=[jax.ShapeDtypeStruct((width,nq),jnp.bfloat16),jax.ShapeDtypeStruct((nk,width),jnp.bfloat16),jax.ShapeDtypeStruct((nk,width),jnp.bfloat16)],interpret=interpret)(qa,k,v,kb,do,o)


epsilon = 1e-06
mask_depth = 1000.0
root_half = 0.7071067811865476
inv_root_tau = 0.3989422804014327


def normalize(matrix):
    average = jnp.mean(matrix, axis=-1, keepdims=True)
    centred = matrix - average
    variance = jnp.mean(centred * centred, axis=-1, keepdims=True)
    inverse = lax.rsqrt(variance + epsilon)
    return (centred * inverse, inverse)


def norm_back(d_normed, gain_row, normed_hat, inverse):
    d_hat = d_normed * gain_row
    first = jnp.mean(d_hat, axis=-1, keepdims=True)
    second = jnp.mean(d_hat * normed_hat, axis=-1, keepdims=True)
    return inverse * (d_hat - first - normed_hat * second)


def gelu_slope(upper):
    return 0.5 * (1.0 + lax.erf(upper * root_half)) + upper * inv_root_tau * jnp.exp(
        -0.5 * upper * upper
    )


def shift_seq(array, step):
    groups = lax.axis_size("seq")
    return lax.ppermute(array, "seq", [(i, (i + step) % groups) for i in range(groups)])


def gather_rows(shard):
    return lax.all_gather(shard, "fsdp", axis=0, tiled=True)


def scatter_rows(grad):
    part = lax.psum_scatter(
        grad.astype(jnp.bfloat16), "fsdp", scatter_dimension=0, tiled=True
    )
    return lax.psum(part, "seq").astype(jnp.float32)


def local(
    tokens,
    teacher,
    out_grad,
    validity,
    loss_grad,
    ln1_gain,
    ln1_bias,
    qkv_weight,
    qv_bias,
    proj_weight,
    proj_bias,
    ln2_gain,
    ln2_bias,
    fc1_weight,
    fc1_bias,
    fc2_weight,
    fc2_bias,
):
    bf16 = jnp.bfloat16
    f32 = jnp.float32
    groups = lax.axis_size("seq")
    shards = lax.axis_size("fsdp")
    clip_count, rows, width = tokens.shape
    assert clip_count == 1
    piece = width // shards
    hidden = fc1_bias.shape[0] * shards
    x_own = tokens.reshape(rows, width)
    valid_own = validity.astype(f32).reshape(rows, 1)

    x_all = jnp.concatenate([x_own] + [shift_seq(x_own, -k) for k in range(1, groups)])
    valid_low = valid_own.astype(bf16).reshape(1, rows)
    valid_all = jnp.concatenate(
        [valid_low] + [shift_seq(valid_low, -k) for k in range(1, groups)], axis=1
    ).astype(f32)
    clip_valid = jnp.sum(valid_all)
    tens = jnp.floor(clip_valid / 16.0)
    vectors = jnp.concatenate(
        [
            ln1_gain,
            ln1_bias,
            qv_bias.reshape(-1),
            proj_bias,
            ln2_gain,
            ln2_bias,
            fc2_bias,
            fc1_bias,
            jnp.stack([tens, clip_valid - 16.0 * tens]).astype(bf16),
            jnp.zeros((126 - 0,), bf16),
        ]
    )
    packed = lax.all_gather(vectors, "fsdp", axis=0).astype(f32)

    def vector(slot):
        return packed[:, slot * piece : (slot + 1) * piece].reshape(1, width)

    gain_one, bias_one, query_bias, value_bias = vector(0), vector(1), vector(2), vector(3)
    proj_shift, gain_two, bias_two, fc2_shift = vector(4), vector(5), vector(6), vector(7)
    tail = 8 * piece
    fc1_shift = packed[:, tail : tail + hidden // shards].reshape(1, hidden)
    tail = tail + hidden // shards
    count = jnp.sum(packed[:, tail] * 16.0 + packed[:, tail + 1])

    qkv_full = gather_rows(qkv_weight)
    proj_full = gather_rows(proj_weight)
    fc1_full = gather_rows(fc1_weight)
    fc2_full = gather_rows(fc2_weight)

    hat_all, inverse_all = normalize(x_all.astype(f32))
    normed_all = (hat_all * gain_one + bias_one).astype(bf16)
    hat_one, inverse_one, normed_one = hat_all[:rows], inverse_all[:rows], normed_all[:rows]
    query = (
        jnp.dot(normed_one, qkv_full[:, :width], preferred_element_type=f32) + query_bias
    ).astype(bf16)
    key = jnp.dot(
        normed_all, qkv_full[:, width : 2 * width], preferred_element_type=f32
    ).astype(bf16)
    value = (
        jnp.dot(normed_all, qkv_full[:, 2 * width :], preferred_element_type=f32) + value_bias
    ).astype(bf16)
    key_bias = jnp.broadcast_to(
        ((valid_all - 1.0) * mask_depth).reshape(-1, 1), (groups * rows, LANES)
    ).astype(bf16)
    attended, query_aug = attn_fwd(query, key, value, key_bias)

    inputs = x_own.astype(f32)
    branch = jnp.dot(attended, proj_full, preferred_element_type=f32) + proj_shift
    resid = inputs + branch
    hat_two, inverse_two = normalize(resid)
    normed_two = (hat_two * gain_two + bias_two).astype(bf16)
    upper = jnp.dot(normed_two, fc1_full, preferred_element_type=f32) + fc1_shift
    active = (0.5 * upper * (1.0 + lax.erf(upper * root_half))).astype(bf16)
    branch_two = jnp.dot(active, fc2_full, preferred_element_type=f32) + fc2_shift
    final = valid_own * (resid + branch_two)
    layer_out = final.reshape(clip_count, rows, width).astype(bf16)
    error = final - teacher.reshape(rows, width).astype(f32)
    error_sum = jnp.sum(valid_own * error * error)
    d_final = (
        out_grad.reshape(rows, width).astype(f32) + loss_grad * 2.0 * valid_own * error / count
    )
    d_inner = valid_own * d_final

    d_out_low = d_inner.astype(bf16)
    grad_fc2 = jnp.einsum("rf,rd->fd", active, d_out_low, preferred_element_type=f32)
    share_fc2 = scatter_rows(grad_fc2)
    grad_fc2_bias = jnp.sum(d_out_low.astype(f32), axis=0)
    d_active = jnp.einsum("rd,fd->rf", d_out_low, fc2_full, preferred_element_type=f32)
    d_upper = (d_active * gelu_slope(upper)).astype(bf16)
    grad_fc1 = jnp.einsum("rd,rf->df", normed_two, d_upper, preferred_element_type=f32)
    share_fc1 = scatter_rows(grad_fc1)
    grad_fc1_bias = jnp.sum(d_upper.astype(f32), axis=0)
    d_normed_two = jnp.einsum("rf,df->rd", d_upper, fc1_full, preferred_element_type=f32)
    grad_gain_two = jnp.sum(d_normed_two * hat_two, axis=0)
    grad_bias_two = jnp.sum(d_normed_two, axis=0)
    d_resid = d_inner + norm_back(d_normed_two, gain_two, hat_two, inverse_two)
    d_branch = d_resid.astype(bf16)
    grad_proj = jnp.einsum("rc,rd->cd", attended, d_branch, preferred_element_type=f32)
    share_proj = scatter_rows(grad_proj)
    grad_proj_bias = jnp.sum(d_branch.astype(f32), axis=0)
    d_attended = jnp.einsum(
        "rd,cd->rc", d_branch, proj_full, preferred_element_type=f32
    ).astype(bf16)

    d_query, d_key, d_value = attn_bwd(
        query_aug, key, value, key_bias, d_attended, attended
    )
    d_pair = jnp.einsum(
        "kc,dc->kd", d_key, qkv_full[:, width : 2 * width], preferred_element_type=f32
    ) + jnp.einsum("kc,dc->kd", d_value, qkv_full[:, 2 * width :], preferred_element_type=f32)
    from_others = [
        shift_seq(d_pair[k * rows : (k + 1) * rows].astype(bf16), k) for k in range(1, groups)
    ]
    grad_query_w = jnp.einsum("rd,cr->dc", normed_one, d_query, preferred_element_type=f32)
    grad_key_w = jnp.einsum("rd,rc->dc", normed_all, d_key, preferred_element_type=f32)
    grad_value_w = jnp.einsum("rd,rc->dc", normed_all, d_value, preferred_element_type=f32)
    share_qkv = scatter_rows(
        jnp.concatenate(
            [grad_query_w.astype(bf16), grad_key_w.astype(bf16), grad_value_w.astype(bf16)], axis=1
        )
    )
    grad_query_bias = jnp.sum(d_query.astype(f32), axis=1)
    grad_value_bias = jnp.sum(d_value.astype(f32), axis=0)
    d_normed_one = d_pair[:rows] + jnp.einsum(
        "cr,dc->rd", d_query, qkv_full[:, :width], preferred_element_type=f32
    )
    for other in from_others:
        d_normed_one = d_normed_one + other.astype(f32)
    grad_gain_one = jnp.sum(d_normed_one * hat_one, axis=0)
    grad_bias_one = jnp.sum(d_normed_one, axis=0)
    d_inputs = d_resid + norm_back(d_normed_one, gain_one, hat_one, inverse_one)
    input_grad = d_inputs.reshape(clip_count, rows, width).astype(bf16)

    vector_grads = jnp.stack(
        [
            grad_gain_one,
            grad_bias_one,
            grad_query_bias,
            grad_value_bias,
            grad_proj_bias,
            grad_gain_two,
            grad_bias_two,
            grad_fc2_bias,
        ]
    )
    vector_grads = jnp.concatenate(
        [
            vector_grads.reshape(8, shards, piece).transpose(1, 0, 2).reshape(shards, 8 * piece),
            grad_fc1_bias.reshape(shards, hidden // shards),
            jnp.broadcast_to(error_sum.reshape(1, 1), (shards, LANES)),
        ],
        axis=1,
    )
    mine = lax.psum_scatter(vector_grads, "fsdp", scatter_dimension=0, tiled=True)
    mine = lax.psum(mine, "seq")[0]
    loss = mine[-1] / count

    def share(slot):
        return mine[slot * piece : (slot + 1) * piece]

    return (
        loss,
        layer_out,
        input_grad,
        share(0),
        share(1),
        share_qkv,
        jnp.stack([share(2), share(3)]),
        share_proj,
        share(4),
        share(5),
        share(6),
        share_fc1,
        mine[8 * piece : 8 * piece + hidden // shards],
        share_fc2,
        share(7),
    )


def solution(mesh):
    placed = (
        P("fsdp", "seq", None),
        P("fsdp", "seq", None),
        P("fsdp", "seq", None),
        P("fsdp", "seq"),
        P(),
        P("fsdp"),
        P("fsdp"),
        P("fsdp", None),
        P(None, "fsdp"),
        P("fsdp", None),
        P("fsdp"),
        P("fsdp"),
        P("fsdp"),
        P("fsdp", None),
        P("fsdp"),
        P("fsdp", None),
        P("fsdp"),
    )
    return jax.shard_map(
        local,
        mesh=mesh,
        in_specs=placed,
        out_specs=(
            P(),
            P("fsdp", "seq", None),
            P("fsdp", "seq", None),
            P("fsdp"),
            P("fsdp"),
            P("fsdp", None),
            P(None, "fsdp"),
            P("fsdp", None),
            P("fsdp"),
            P("fsdp"),
            P("fsdp"),
            P("fsdp", None),
            P("fsdp"),
            P("fsdp", None),
            P("fsdp"),
        ),
        check_vma=False,
    )
```

```python
import jax
import jax.numpy as jnp
from jax import lax
from jax.experimental import pallas as pl
from jax.experimental.pallas import tpu as pltpu
from jax.sharding import PartitionSpec as P


LANES=128

DH=64


def lane_of(n): return lax.broadcasted_iota(jnp.int32,(n,LANES),1)


NT=(((1,),(1,)),((),()))
NN=(((1,),(0,)),((),()))


def mm(a,b,d): return lax.dot_general(a,b,d,preferred_element_type=jnp.float32)


def split3(col):
    hi=col.astype(jnp.bfloat16).astype(jnp.float32)
    rest=col-hi
    mid=rest.astype(jnp.bfloat16).astype(jnp.float32)
    return hi,mid,rest-mid


def key_side(k,kb,lane,h):
    base=DH*(1-h)
    extra=jnp.where(lane==base,kb,jnp.where((lane>base)&(lane<base+4),1.0,0.0))
    return jnp.where(lane//DH==h,k,extra).astype(jnp.bfloat16)


def fwd_kernel(q_ref,k_ref,v_ref,kb_ref,o_ref,qa_ref,*,chunk):
    nq=q_ref.shape[0]; nk=k_ref.shape[0]
    lane_k=lane_of(nk); lane_q=lane_of(chunk)
    k=k_ref[...].astype(jnp.float32); v=v_ref[...].astype(jnp.float32); kb=kb_ref[...].astype(jnp.float32)
    keys=[key_side(k,kb,lane_k,h) for h in (0,1)]
    vals=[jnp.where(lane_k//DH==h,v,jnp.where(lane_k==DH*(1-h),1.0,0.0)).astype(jnp.bfloat16) for h in (0,1)]
    for c in range(nq//chunk):
        rows=pl.ds(c*chunk,chunk)
        q=q_ref[rows,:].astype(jnp.float32)*0.125
        outs=[]
        for h in (0,1):
            base=DH*(1-h)
            inh=lane_q//DH==h
            qh=jnp.where(inh,q,jnp.where(lane_q==base,1.0,0.0))
            s=mm(qh.astype(jnp.bfloat16),keys[h],NT)
            m=jnp.max(s,axis=1,keepdims=True)
            p=jnp.exp(s-m).astype(jnp.bfloat16)
            o=mm(p,vals[h],NN)
            l=o[:,base:base+1]
            outs.append(o/l)
            hi,mid,lo=split3(m+jnp.log(l))
            qa=jnp.where(lane_q==base+1,-hi,jnp.where(lane_q==base+2,-mid,jnp.where(lane_q==base+3,-lo,qh)))
            qa_ref[rows,h*LANES:(h+1)*LANES]=qa.astype(jnp.bfloat16)
        o_ref[rows,:]=jnp.where(lane_q<DH,outs[0],outs[1]).astype(jnp.bfloat16)


def bwd_kernel(qa_ref,k_ref,v_ref,kb_ref,do_ref,o_ref,dq_ref,dk_ref,dv_ref,*,chunk):
    nq=do_ref.shape[0]; nk=k_ref.shape[0]
    lane_q=lane_of(nq); lane_k=lane_of(chunk)
    do=do_ref[...].astype(jnp.float32)
    prod=do*o_ref[...].astype(jnp.float32)
    dos=[];
    for h in (0,1):
        base=DH*(1-h)
        inh=lane_q//DH==h
        d=jnp.sum(jnp.where(inh,prod,0.0),axis=1,keepdims=True)
        hi,mid,lo=split3(d)
        dos.append(jnp.where(inh,do,jnp.where(lane_q==base,-hi,jnp.where(lane_q==base+1,-mid,jnp.where(lane_q==base+2,-lo,0.0)))).astype(jnp.bfloat16))
    dq=[None,None]
    for c in range(nk//chunk):
        rows=pl.ds(c*chunk,chunk)
        k=k_ref[rows,:].astype(jnp.float32); v=v_ref[rows,:].astype(jnp.float32); kb=kb_ref[rows,:].astype(jnp.float32)
        kt=k.T.astype(jnp.bfloat16)
        dks=[];dvs=[]
        for h in (0,1):
            base=DH*(1-h)
            inh=lane_k//DH==h
            qa=qa_ref[:,h*LANES:(h+1)*LANES]
            ka=key_side(k,kb,lane_k,h)
            va=jnp.where(inh,v,jnp.where((lane_k>=base)&(lane_k<base+3),1.0,0.0)).astype(jnp.bfloat16)
            p=jnp.exp(mm(ka,qa,NT))
            dp=mm(va,dos[h],NT)
            ds=(p*dp).astype(jnp.bfloat16)
            dvs.append(mm(p.astype(jnp.bfloat16),dos[h],NN))
            dks.append(mm(ds,qa,NN))
            part=mm(kt[h*DH:(h+1)*DH,:],ds,NN)
            dq[h]=part if dq[h] is None else dq[h]+part
        dk_ref[rows,:]=jnp.where(lane_k<DH,dks[0],dks[1]).astype(jnp.bfloat16)
        dv_ref[rows,:]=jnp.where(lane_k<DH,dvs[0],dvs[1]).astype(jnp.bfloat16)
    for h in (0,1):
        dq_ref[h*DH:(h+1)*DH,:]=(dq[h]*0.125).astype(jnp.bfloat16)


def attn_fwd(q,k,v,kb,interpret=False):
    nq,width=q.shape; nk=k.shape[0]; pairs=width//LANES
    chunk=min(256,nq)
    return pl.pallas_call(lambda *r:fwd_kernel(*r,chunk=chunk),grid=(pairs,),
      in_specs=[pl.BlockSpec((nq,LANES),lambda i:(0,i)),pl.BlockSpec((nk,LANES),lambda i:(0,i)),pl.BlockSpec((nk,LANES),lambda i:(0,i)),pl.BlockSpec((nk,LANES),lambda i:(0,0))],
      out_specs=[pl.BlockSpec((nq,LANES),lambda i:(0,i)),pl.BlockSpec((nq,2*LANES),lambda i:(0,i))],
      out_shape=[jax.ShapeDtypeStruct((nq,width),jnp.bfloat16),jax.ShapeDtypeStruct((nq,2*width),jnp.bfloat16)],interpret=interpret)(q,k,v,kb)


def attn_bwd(qa,k,v,kb,do,o,interpret=False):
    nq,width=do.shape; nk=k.shape[0]; pairs=width//LANES
    chunk=min(256,nk)
    return pl.pallas_call(lambda *r:bwd_kernel(*r,chunk=chunk),grid=(pairs,),
      in_specs=[pl.BlockSpec((nq,2*LANES),lambda i:(0,i)),pl.BlockSpec((nk,LANES),lambda i:(0,i)),pl.BlockSpec((nk,LANES),lambda i:(0,i)),pl.BlockSpec((nk,LANES),lambda i:(0,0)),pl.BlockSpec((nq,LANES),lambda i:(0,i)),pl.BlockSpec((nq,LANES),lambda i:(0,i))],
      out_specs=[pl.BlockSpec((LANES,nq),lambda i:(i,0)),pl.BlockSpec((nk,LANES),lambda i:(0,i)),pl.BlockSpec((nk,LANES),lambda i:(0,i))],
      out_shape=[jax.ShapeDtypeStruct((width,nq),jnp.bfloat16),jax.ShapeDtypeStruct((nk,width),jnp.bfloat16),jax.ShapeDtypeStruct((nk,width),jnp.bfloat16)],interpret=interpret)(qa,k,v,kb,do,o)


BOTH = ("fsdp", "seq")


def place():
    f = lax.axis_index("fsdp")
    return f // 4, (f // 2) % 2, f % 2, lax.axis_index("seq")


def send(array, dz=0, dx=0, dc=0, dy=0):
    pairs = []
    for z in range(4):
        for x in range(2):
            for c in range(2):
                for y in range(2):
                    step = dz[y] if isinstance(dz, tuple) else dz
                    to = ((z ^ step) * 4 + (x ^ dx) * 2 + (c ^ dc)) * 2 + (y ^ dy)
                    pairs.append(((z * 4 + x * 2 + c) * 2 + y, to))
    return lax.ppermute(array, BOTH, pairs)


def assemble_kernel(where_ref, *refs, groups, rows):
    n = len(groups)
    split = len(refs) - n == 6
    outs = refs[n : n + 1 + split]
    bufs = refs[n + 1 + split : n + 2 + 2 * split]
    sem_in, sem_out = refs[-2:]
    loads = []
    at = 0
    for size, ref in zip(groups, refs[:n]):
        for j in range(size):
            spot = where_ref[at]
            for t in range(1 + split):
                part = ref.at[j]
                if split:
                    part = ref.at[j, pl.ds(0, rows) if t == 0 else pl.ds(rows, ref.shape[1] - rows)]
                load = pltpu.make_async_copy(part, bufs[t].at[spot], sem_in.at[t, at])
                load.start()
                loads.append((load, t, spot, at))
            at += 1
    stores = []
    for load, t, spot, i in loads:
        load.wait()
        store = pltpu.make_async_copy(bufs[t].at[spot], outs[t].at[spot], sem_out.at[t, i])
        store.start()
        stores.append(store)
    for store in stores:
        store.wait()


def assemble(pieces, where, rows):
    groups = tuple(p.shape[0] for p in pieces)
    n = sum(groups)
    total, width = pieces[0].shape[1:]
    anywhere = pl.BlockSpec(memory_space=pl.ANY)
    shapes = [(n, rows, width)] + ([(n, total - rows, width)] if total > rows else [])
    dtype = pieces[0].dtype
    return pl.pallas_call(
        lambda *refs: assemble_kernel(*refs, groups=groups, rows=rows),
        in_specs=[pl.BlockSpec(memory_space=pltpu.SMEM)] + [anywhere] * len(pieces),
        out_specs=[anywhere] * len(shapes),
        out_shape=[jax.ShapeDtypeStruct(s, dtype) for s in shapes],
        scratch_shapes=[pltpu.VMEM(s, dtype) for s in shapes]
        + [
            pltpu.SemaphoreType.DMA((len(shapes), n)),
            pltpu.SemaphoreType.DMA((len(shapes), n)),
        ],
    )(where, *pieces)


def finish(pieces, index, core_major, rows):
    c = lax.axis_index("fsdp") % 2
    other = [send(p, dc=1) for p in pieces]
    if core_major:
        where = [c * 8 + i for i in index] + [(1 - c) * 8 + i for i in index]
    else:
        where = [2 * i + c for i in index] + [2 * i + 1 - c for i in index]
    outs = assemble(pieces + other, jnp.stack(where).astype(jnp.int32), rows or pieces[0].shape[1])
    full = outs[0].reshape((-1,) + outs[0].shape[2:])
    return (full, outs[1][:, 0, :]) if len(outs) > 1 else full


def gather_flat(own, core_major=False):
    z, x, _, _ = place()
    own = own[None]
    head = send(own, dx=1)
    two = send(own, dz=2)
    pair = send(jnp.concatenate([own, two]), dz=1)
    rest = send(jnp.concatenate([two, pair]), dx=1)
    index = [(z ^ r) * 2 + (x ^ k) for k in (0, 1) for r in (0, 2, 1, 3)]
    return finish([own, two, pair, head, rest], index, core_major, None)


def gather_shared(own, core_major=False, rows=None):
    z, x, _, y = place()
    own = own[None]
    a = send(own, dz=1)
    b = send(own, dz=(2, 3))
    xs = send(jnp.concatenate([jnp.where(y == 0, own, a), b]), dx=1)
    ys = send(jnp.concatenate([b, xs]), dy=1)
    near = z * 2 + x
    index = [
        near,
        (z ^ 1) * 2 + x,
        (z ^ (2 + y)) * 2 + x,
        (z ^ y) * 2 + (x ^ 1),
        (z ^ (2 + y)) * 2 + (x ^ 1),
        (z ^ (3 - y)) * 2 + x,
        (z ^ (1 - y)) * 2 + (x ^ 1),
        (z ^ (3 - y)) * 2 + (x ^ 1),
    ]
    return finish([own, a, b, xs, ys], index, core_major, rows)


def pick(a, i):
    return lax.dynamic_index_in_dim(a, i, 0, keepdims=False)


def pick_second(a, i):
    return lax.dynamic_index_in_dim(a, i, 1, keepdims=False)


def add(*xs):
    total = xs[0].astype(jnp.float32)
    for other in xs[1:]:
        total = total + other.astype(jnp.float32)
    return total.astype(jnp.bfloat16)


def scatter_flat(keep, give):
    z, x, _, _ = place()
    got = send(give, dc=1)
    keep4 = keep.reshape((4, 2) + keep.shape[1:])
    got4 = got.reshape((4, 2) + got.shape[1:])
    gx = send(add(pick_second(keep4, 1 - x), pick_second(got4, 1 - x)), dx=1)

    def part(k, *more):
        i = (z ^ k) * 2 + x
        return add(pick(keep, i), pick(got, i), pick(gx, z ^ k), *more)

    pair = send(jnp.stack([part(1), part(3)]), dz=1)
    far = send(part(2, pair[1]), dz=2)
    o = part(0, pair[0], far)
    return o.astype(jnp.float32) + send(o, dy=1).astype(jnp.float32)


def scatter_shared(keep, give):
    z, x, _, y = place()
    got = send(give, dc=1)

    def chunk(dz, dx, *more):
        i = (z ^ dz) * 2 + (x ^ dx)
        return add(pick(keep, i), pick(got, i), *more)

    ys = send(jnp.stack([chunk(1 - y, 1), chunk(3 - y, 1), chunk(3 - y, 0)]), dy=1)
    xs = send(jnp.stack([chunk(y, 1, ys[0]), chunk(2 + y, 1, ys[1])]), dx=1)
    first = xs[0].astype(jnp.float32)
    a = send(chunk(1, 0, first * (y == 1)), dz=1)
    b = send(chunk(2 + y, 0, ys[2], xs[1]), dz=(2, 3))
    o = chunk(0, 0, first * (y == 0), a, b)
    return o.astype(jnp.float32) + send(o, dy=1).astype(jnp.float32)


def scatter_vectors(grads):
    z, x, c, _ = place()
    grads = grads.reshape(8, 2, 8, 128)
    eight = pick_second(grads, c) + send(pick_second(grads, 1 - c), dc=1)
    eight = eight.reshape(4, 2, 8, 128)
    four = pick_second(eight, x) + send(pick_second(eight, 1 - x), dx=1)
    total = pick(four, z)
    for k in (1, 2, 3):
        total = total + send(pick(four, z ^ k), dz=k)
    return total + send(total, dy=1)


epsilon = 1e-06
mask_depth = 1000.0
root_half = 0.7071067811865476
inv_root_tau = 0.3989422804014327


def normalize(matrix):
    average = jnp.mean(matrix, axis=-1, keepdims=True)
    centred = matrix - average
    variance = jnp.mean(centred * centred, axis=-1, keepdims=True)
    inverse = lax.rsqrt(variance + epsilon)
    return (centred * inverse, inverse)


def norm_back(d_normed, gain_row, normed_hat, inverse):
    d_hat = d_normed * gain_row
    first = jnp.mean(d_hat, axis=-1, keepdims=True)
    second = jnp.mean(d_hat * normed_hat, axis=-1, keepdims=True)
    return inverse * (d_hat - first - normed_hat * second)


def gelu_slope(upper):
    return 0.5 * (1.0 + lax.erf(upper * root_half)) + upper * inv_root_tau * jnp.exp(
        -0.5 * upper * upper
    )


def shift_seq(array, step):
    groups = lax.axis_size("seq")
    return lax.ppermute(array, "seq", [(i, (i + step) % groups) for i in range(groups)])


def gather_rows(shard):
    return lax.all_gather(shard, "fsdp", axis=0, tiled=True)


def halves(array, core):
    width = array.shape[1]
    unit = width // 16
    column = lax.broadcasted_iota(jnp.int32, (width, width), 1)
    row = lax.broadcasted_iota(jnp.int32, (width, width), 0)
    local_column = column % (width // 2)
    owner = jnp.where(column < width // 2, core, 1 - core)
    source = (local_column // unit) * (2 * unit) + owner * unit + local_column % unit
    chosen = (row == source).astype(jnp.bfloat16)
    return jnp.dot(array, chosen, preferred_element_type=jnp.float32).astype(jnp.bfloat16)


def core_major(array):
    lead = array.shape[:-1]
    unit = array.shape[-1] // 16
    return array.reshape(lead + (8, 2, unit)).swapaxes(-3, -2).reshape(array.shape)


def core_minor(array):
    lead = array.shape[:-1]
    unit = array.shape[-1] // 16
    return array.reshape(lead + (2, 8, unit)).swapaxes(-3, -2).reshape(array.shape)


def row_blocks(grad):
    return grad.astype(jnp.bfloat16).reshape(8, grad.shape[0] // 8, grad.shape[1])


def scatter_rows(grad):
    part = lax.psum_scatter(
        grad.astype(jnp.bfloat16), "fsdp", scatter_dimension=0, tiled=True
    )
    return lax.psum(part, "seq").astype(jnp.float32)


def local(
    tokens,
    teacher,
    out_grad,
    validity,
    loss_grad,
    ln1_gain,
    ln1_bias,
    qkv_weight,
    qv_bias,
    proj_weight,
    proj_bias,
    ln2_gain,
    ln2_bias,
    fc1_weight,
    fc1_bias,
    fc2_weight,
    fc2_bias,
):
    bf16 = jnp.bfloat16
    f32 = jnp.float32
    groups = lax.axis_size("seq")
    shards = lax.axis_size("fsdp")
    clip_count, rows, width = tokens.shape
    assert clip_count == 1
    piece = width // shards
    hidden = fc1_bias.shape[0] * shards
    routed = shards == 16 and groups == 2
    x_own = tokens.reshape(rows, width)
    valid_own = validity.astype(f32).reshape(rows, 1)

    valid_low = valid_own.astype(bf16).reshape(1, rows)
    valid_others = [shift_seq(valid_low, -k) for k in range(1, groups)]
    x_others = [shift_seq(x_own, -k) for k in range(1, groups)]
    valid_all = jnp.concatenate([valid_low] + valid_others, axis=1).astype(f32)
    clip_valid = jnp.sum(valid_all)
    tens = jnp.floor(clip_valid / 16.0)
    vectors = jnp.concatenate(
        [
            ln1_gain,
            ln1_bias,
            qv_bias.reshape(-1),
            proj_bias,
            ln2_gain,
            ln2_bias,
            fc2_bias,
            fc1_bias,
            jnp.stack([tens, clip_valid - 16.0 * tens]).astype(bf16),
        ]
    )
    vectors = jnp.pad(vectors, (0, 1024 - vectors.shape[0]))
    if routed:
        led = jnp.concatenate(
            [qkv_weight[:, :width], jnp.broadcast_to(vectors[None, :], (16, width))]
        )
        query_w, packed = gather_shared(led, rows=piece)
        packed = packed.astype(f32)
        key_w = gather_shared(qkv_weight[:, width : 2 * width])
        value_w = gather_shared(qkv_weight[:, 2 * width :])
        fc1_full = gather_shared(core_major(fc1_weight))
        proj_full = gather_flat(proj_weight)
        fc2_full = gather_flat(fc2_weight, core_major=True)
    else:
        packed = lax.all_gather(vectors, "fsdp", axis=0).astype(f32)
        qkv_full = gather_rows(qkv_weight)
        query_w, key_w, value_w = jnp.split(qkv_full, 3, axis=1)
        proj_full = gather_rows(proj_weight)
        fc1_full = gather_rows(fc1_weight)
        fc2_full = gather_rows(fc2_weight)

    def vector(slot):
        return packed[:, slot * piece : (slot + 1) * piece].reshape(1, width)

    gain_one, bias_one, query_bias, value_bias = vector(0), vector(1), vector(2), vector(3)
    proj_shift, gain_two, bias_two, fc2_shift = vector(4), vector(5), vector(6), vector(7)
    tail = 8 * piece
    fc1_shift = packed[:, tail : tail + hidden // shards].reshape(1, hidden)
    if routed:
        fc1_shift = core_major(fc1_shift)
    tail = tail + hidden // shards
    count = jnp.sum(packed[:, tail] * 16.0 + packed[:, tail + 1])

    hat_one, inverse_one = normalize(x_own.astype(f32))
    normed_one = (hat_one * gain_one + bias_one).astype(bf16)
    normed_all = jnp.concatenate(
        [normed_one]
        + [(normalize(x.astype(f32))[0] * gain_one + bias_one).astype(bf16) for x in x_others]
    )
    query = (
        jnp.dot(normed_one, query_w, preferred_element_type=f32) + query_bias
    ).astype(bf16)
    key = jnp.dot(normed_all, key_w, preferred_element_type=f32).astype(bf16)
    value = (
        jnp.dot(normed_all, value_w, preferred_element_type=f32) + value_bias
    ).astype(bf16)
    key_bias = jnp.broadcast_to(
        ((valid_all - 1.0) * mask_depth).reshape(-1, 1), (groups * rows, LANES)
    ).astype(bf16)
    attended, query_aug = attn_fwd(query, key, value, key_bias)
    core = lax.axis_index("fsdp") % 2
    half = width // 2
    if routed:
        split_all = halves(normed_all, core)
        split_attended = halves(attended, core)

    inputs = x_own.astype(f32)
    branch = jnp.dot(attended, proj_full, preferred_element_type=f32) + proj_shift
    resid = inputs + branch
    hat_two, inverse_two = normalize(resid)
    normed_two = (hat_two * gain_two + bias_two).astype(bf16)
    if routed:
        split_two = halves(normed_two, core)
    upper = jnp.dot(normed_two, fc1_full, preferred_element_type=f32) + fc1_shift
    active = (0.5 * upper * (1.0 + lax.erf(upper * root_half))).astype(bf16)
    branch_two = jnp.dot(active, fc2_full, preferred_element_type=f32) + fc2_shift
    final = valid_own * (resid + branch_two)
    layer_out = final.reshape(clip_count, rows, width).astype(bf16)
    error = final - teacher.reshape(rows, width).astype(f32)
    error_sum = jnp.sum(valid_own * error * error)
    d_final = (
        out_grad.reshape(rows, width).astype(f32) + loss_grad * 2.0 * valid_own * error / count
    )
    d_inner = valid_own * d_final

    d_out_low = d_inner.astype(bf16)
    if routed:

        def fc2_half(side):
            left = lax.dynamic_slice(active, (0, side * (hidden // 2)), (rows, hidden // 2))
            grad = jnp.einsum("rf,rd->fd", left, d_out_low, preferred_element_type=f32)
            return row_blocks(grad)

        share_fc2 = scatter_shared(fc2_half(core), fc2_half(1 - core))
    else:
        grad_fc2 = jnp.einsum("rf,rd->fd", active, d_out_low, preferred_element_type=f32)
        share_fc2 = scatter_rows(grad_fc2)
    grad_fc2_bias = jnp.sum(d_out_low.astype(f32), axis=0)
    d_active = jnp.einsum("rd,fd->rf", d_out_low, fc2_full, preferred_element_type=f32)
    d_upper = (d_active * gelu_slope(upper)).astype(bf16)
    if routed:
        def fc1_half(left):
            return row_blocks(
                jnp.einsum("rd,rf->df", left, d_upper, preferred_element_type=f32)
            )

        share_fc1 = scatter_flat(fc1_half(split_two[:, :half]), fc1_half(split_two[:, half:]))
        share_fc1 = core_minor(share_fc1)
    else:
        grad_fc1 = jnp.einsum("rd,rf->df", normed_two, d_upper, preferred_element_type=f32)
        share_fc1 = scatter_rows(grad_fc1)
    grad_fc1_bias = jnp.sum(d_upper.astype(f32), axis=0)
    d_normed_two = jnp.einsum("rf,df->rd", d_upper, fc1_full, preferred_element_type=f32)
    grad_gain_two = jnp.sum(d_normed_two * hat_two, axis=0)
    grad_bias_two = jnp.sum(d_normed_two, axis=0)
    d_resid = d_inner + norm_back(d_normed_two, gain_two, hat_two, inverse_two)
    d_branch = d_resid.astype(bf16)
    if routed:
        share_proj = scatter_flat(
            row_blocks(jnp.einsum("rc,rd->cd", split_attended[:, :half], d_branch, preferred_element_type=f32)),
            row_blocks(jnp.einsum("rc,rd->cd", split_attended[:, half:], d_branch, preferred_element_type=f32)),
        )
    else:
        grad_proj = jnp.einsum("rc,rd->cd", attended, d_branch, preferred_element_type=f32)
        share_proj = scatter_rows(grad_proj)
    grad_proj_bias = jnp.sum(d_branch.astype(f32), axis=0)
    d_attended = jnp.einsum(
        "rd,cd->rc", d_branch, proj_full, preferred_element_type=f32
    ).astype(bf16)

    d_query, d_key, d_value = attn_bwd(
        query_aug, key, value, key_bias, d_attended, attended
    )

    def back_kv(first, last):
        return jnp.einsum(
            "kc,dc->kd", d_key[first:last], key_w, preferred_element_type=f32
        ) + jnp.einsum("kc,dc->kd", d_value[first:last], value_w, preferred_element_type=f32)

    from_others = [
        shift_seq(back_kv(k * rows, (k + 1) * rows).astype(bf16), k)
        for k in range(1, groups)
    ]
    if routed:

        def qkv_half(form, left, right):
            return row_blocks(jnp.einsum(form, left, right, preferred_element_type=f32))

        share_qkv = jnp.concatenate(
            [
                scatter_shared(
                    qkv_half("rd,cr->dc", split_all[:rows, :half], d_query),
                    qkv_half("rd,cr->dc", split_all[:rows, half:], d_query),
                ),
                scatter_flat(
                    qkv_half("rd,rc->dc", split_all[:, :half], d_key), qkv_half("rd,rc->dc", split_all[:, half:], d_key)
                ),
                scatter_shared(
                    qkv_half("rd,rc->dc", split_all[:, :half], d_value),
                    qkv_half("rd,rc->dc", split_all[:, half:], d_value),
                ),
            ],
            axis=1,
        )
    else:
        grad_query_w = jnp.einsum("rd,cr->dc", normed_one, d_query, preferred_element_type=f32)
        grad_key_w = jnp.einsum("rd,rc->dc", normed_all, d_key, preferred_element_type=f32)
        grad_value_w = jnp.einsum("rd,rc->dc", normed_all, d_value, preferred_element_type=f32)
        share_qkv = scatter_rows(
            jnp.concatenate(
                [grad_query_w.astype(bf16), grad_key_w.astype(bf16), grad_value_w.astype(bf16)],
                axis=1,
            )
        )
    grad_query_bias = jnp.sum(d_query.astype(f32), axis=1)
    grad_value_bias = jnp.sum(d_value.astype(f32), axis=0)
    d_normed_one = back_kv(0, rows) + jnp.einsum(
        "cr,dc->rd", d_query, query_w, preferred_element_type=f32
    )
    for other in from_others:
        d_normed_one = d_normed_one + other.astype(f32)
    grad_gain_one = jnp.sum(d_normed_one * hat_one, axis=0)
    grad_bias_one = jnp.sum(d_normed_one, axis=0)
    d_inputs = d_resid + norm_back(d_normed_one, gain_one, hat_one, inverse_one)
    input_grad = d_inputs.reshape(clip_count, rows, width).astype(bf16)

    vector_grads = jnp.stack(
        [
            grad_gain_one,
            grad_bias_one,
            grad_query_bias,
            grad_value_bias,
            grad_proj_bias,
            grad_gain_two,
            grad_bias_two,
            grad_fc2_bias,
        ]
    )
    fc1_bias_row = core_minor(grad_fc1_bias) if routed else grad_fc1_bias
    used = 8 * piece + hidden // shards
    vector_grads = jnp.concatenate(
        [
            vector_grads.reshape(8, shards, piece).transpose(1, 0, 2).reshape(shards, 8 * piece),
            fc1_bias_row.reshape(shards, hidden // shards),
            jnp.broadcast_to(error_sum.reshape(1, 1), (shards, 1024 - used)),
        ],
        axis=1,
    )
    if routed:
        mine = scatter_vectors(vector_grads).reshape(1024)
    else:
        mine = lax.psum_scatter(vector_grads, "fsdp", scatter_dimension=0, tiled=True)
        mine = lax.psum(mine, "seq")[0]
    loss = mine[-1] / count

    def share(slot):
        return mine[slot * piece : (slot + 1) * piece]

    return (
        loss,
        layer_out,
        input_grad,
        share(0),
        share(1),
        share_qkv,
        jnp.stack([share(2), share(3)]),
        share_proj,
        share(4),
        share(5),
        share(6),
        share_fc1,
        mine[8 * piece : 8 * piece + hidden // shards],
        share_fc2,
        share(7),
    )


def solution(mesh):
    placed = (
        P("fsdp", "seq", None),
        P("fsdp", "seq", None),
        P("fsdp", "seq", None),
        P("fsdp", "seq"),
        P(),
        P("fsdp"),
        P("fsdp"),
        P("fsdp", None),
        P(None, "fsdp"),
        P("fsdp", None),
        P("fsdp"),
        P("fsdp"),
        P("fsdp"),
        P("fsdp", None),
        P("fsdp"),
        P("fsdp", None),
        P("fsdp"),
    )
    return jax.shard_map(
        local,
        mesh=mesh,
        in_specs=placed,
        out_specs=(
            P(),
            P("fsdp", "seq", None),
            P("fsdp", "seq", None),
            P("fsdp"),
            P("fsdp"),
            P("fsdp", None),
            P(None, "fsdp"),
            P("fsdp", None),
            P("fsdp"),
            P("fsdp"),
            P("fsdp"),
            P("fsdp", None),
            P("fsdp"),
            P("fsdp", None),
            P("fsdp"),
        ),
        check_vma=False,
    )
```
